32 devices in a mesh: member: 2 (over y), cell: 16 (over z, x, core).
Axes of the slice: x: 2, y: 2, z: 4, core: 2. Of those that a mesh axis runs over, the one named last changes fastest.
Arguments:
- wave_energy: float32 [2304, 2048], P(('member', 'cell')), parts along dimension 0, may hold values from -6 to 6
- courant: float32 [1152], replicated, may hold values from -0.9 to 0.9
- sea_mask: int32 [2048], replicated, may hold values 0 or 1
- lift_weight: bfloat16 [1024, 1152], replicated, may hold values from -0.1875 to 0.1875
- back_weight: bfloat16 [1152, 1024], replicated, may hold values from -0.1875 to 0.1875
Outputs:
- wave_next: float32 [2304, 2048], P(('member', 'cell')), parts along dimension 0
The draws below stay inside these ranges and needn't reach their ends.
There are 2 independent parts, one for each index of `member`. The reference program is written for one: setup_inputs(seed, part) draws one part's arguments, and reference() takes and returns one part's arrays. A program takes and returns all parts, laid end to end along the dimension named above; an argument that names none is the same for every part. Nothing has to cross between parts.
All inputs are finite; a program needn't handle non-finite values.
Results may differ from the reference program's by a relative error of at most 0.0026.
Values sent between devices are 32-bit elements; how exact they have to be, the bound alone decides.
A program may use at most 64 MiB of HBM per device.

```python
import jax
import jax.numpy as jnp
from jax import lax

K = 1152
R = 1024
CELL_DEV = 128
STEPS = 2
NC = 2048
N_CELL = 16


def place_ends(values, rng, low, high):
    longest = values.shape.index(max(values.shape))
    spots = []
    for shift in (0, 1):
        where = [jax.random.randint(jax.random.fold_in(rng, axis), (), 0, length) for axis, length in enumerate(values.shape)]
        where[longest] = (where[longest] + shift) % values.shape[longest]
        spots.append(tuple(where))
    return values.at[spots[0]].set(low).at[spots[1]].set(high)


def level_of(key, dims, split, smallest, largest):
    gain, own = 1.0, jax.random.fold_in(key, 6)
    for dim, parts in split:
        steps = jnp.exp(jax.random.uniform(jax.random.fold_in(own, dim), (parts,), jnp.float32, smallest / len(split), largest / len(split)))
        gain = gain * jnp.repeat(steps, dims[dim] // parts).reshape([-1 if axis == dim else 1 for axis in range(len(dims))])
    return gain


def bell_draw(key, dims, scale, bound, shards=(), dtype=jnp.bfloat16):
    gain = level_of(key, dims, shards, -0.22, 0.18) if shards else 1.0
    entries = jax.random.normal(key, dims, jnp.float32) * scale * gain
    return jnp.minimum(jnp.maximum(entries, -bound), bound).astype(dtype)


def setup_inputs(seed: int = 0, part: int = 0) -> dict:
    seeds = jax.random.split(jax.random.key(seed), 6)
    part_splits = jax.random.split(jax.random.fold_in(seeds[5], part), 6)
    return {
        "wave_energy": bell_draw(part_splits[0], (K, NC), 1.0, 6.0, ((0, 16),), jnp.float32),
        "courant": jnp.clip(jax.random.uniform(seeds[1], (K,), jnp.float32, -0.9, 0.9), -0.9, 0.9),
        "sea_mask": place_ends((jax.random.randint(seeds[2], (NC,), 0, 10) < 7).astype(jnp.int32), jax.random.fold_in(seeds[2], 1), 0, 1),
        "lift_weight": bell_draw(seeds[3], (R, K), K ** -0.5, 0.1875),
        "back_weight": bell_draw(seeds[4], (K, R), R ** -0.5, 0.1875),
    }


coupling = 0.25


def minmod(first_term, second_term):
    return 0.5 * (jnp.sign(first_term) + jnp.sign(second_term)) * jnp.minimum(jnp.abs(first_term), jnp.abs(second_term))


def substep(spectra, sea_field, speeds):
    extent_cells = spectra.shape[1]
    differences = spectra[:, 1:] - spectra[:, :-1]
    slopes = minmod(differences[:, 1:], differences[:, :-1])
    forward_speed = jnp.maximum(speeds, 0.0)
    backward_speed = jnp.minimum(speeds, 0.0)
    open_faces = sea_field[1:extent_cells - 2] * sea_field[2:extent_cells - 1]
    fluxes = forward_speed * (spectra[:, 1:extent_cells - 2] + 0.5 * (1.0 - forward_speed) * slopes[:, 0:extent_cells - 3])
    fluxes = fluxes + backward_speed * (spectra[:, 2:extent_cells - 1] - 0.5 * (1.0 + backward_speed) * slopes[:, 1:extent_cells - 2])
    fluxes = fluxes * open_faces
    return spectra[:, 2:extent_cells - 2] - (fluxes[:, 1:] - fluxes[:, :-1])


def reference(wave_energy, courant, sea_mask, lift_weight, back_weight):
    sea_field = sea_mask.astype(jnp.float32)
    sea_padded = jnp.pad(sea_field, 2)
    groups = K // N_CELL

    def propagate(inputs):
        block_state, speeds = inputs
        for turn_index in range(2):
            block_state = substep(jnp.pad(block_state, ((0, 0), (2, 2))), sea_padded, speeds[:, None])
        return block_state

    def fourwave(block_state):
        lifted = jnp.dot(lift_weight, block_state.astype(jnp.bfloat16), preferred_element_type=jnp.float32)
        squared = (lifted * lifted).astype(jnp.bfloat16)
        source = jnp.dot(back_weight, squared, preferred_element_type=jnp.float32)
        return block_state + coupling * source

    spectra = wave_energy
    for repeat in range(STEPS):
        spectra = lax.map(propagate, (spectra.reshape(N_CELL, groups, NC), courant.reshape(N_CELL, groups))).reshape(K, NC)
        cell_tiles = spectra.reshape(K, N_CELL, CELL_DEV).transpose(1, 0, 2)
        spectra = lax.map(fourwave, cell_tiles).transpose(1, 0, 2).reshape(K, NC)
    return spectra
```

```python
import jax
import jax.numpy as jnp
from jax import lax
from jax.sharding import PartitionSpec as P

STEPS = 2


coupling = 0.25


def with_halo(value, sides, width):
    for axis, dim in sides:
        devices, length = (lax.axis_size(axis), value.shape[dim])
        up = [(i, (i + 1) % devices) for i in range(devices - 1)]
        down = [(j, i) for i, j in up]
        last = lax.slice_in_dim(value, length - width, length, axis=dim)
        first = lax.slice_in_dim(value, 0, width, axis=dim)
        before = lax.ppermute(last, axis, up)
        after = lax.ppermute(first, axis, down)
        value = jnp.concatenate([before, value, after], axis=dim)
    return value


def minmod(first_term, second_term):
    return (
        0.5
        * (jnp.sign(first_term) + jnp.sign(second_term))
        * jnp.minimum(jnp.abs(first_term), jnp.abs(second_term))
    )


def substep(spectra, sea_field, speeds):
    extent_cells = spectra.shape[1]
    differences = spectra[:, 1:] - spectra[:, :-1]
    slopes = minmod(differences[:, 1:], differences[:, :-1])
    forward_speed = jnp.maximum(speeds, 0.0)
    backward_speed = jnp.minimum(speeds, 0.0)
    open_faces = sea_field[1 : extent_cells - 2] * sea_field[2 : extent_cells - 1]
    fluxes = forward_speed * (
        spectra[:, 1 : extent_cells - 2]
        + 0.5 * (1.0 - forward_speed) * slopes[:, 0 : extent_cells - 3]
    )
    fluxes = fluxes + backward_speed * (
        spectra[:, 2 : extent_cells - 1]
        - 0.5 * (1.0 + backward_speed) * slopes[:, 1 : extent_cells - 2]
    )
    fluxes = fluxes * open_faces
    return spectra[:, 2 : extent_cells - 2] - (fluxes[:, 1:] - fluxes[:, :-1])


def fourwave(state, lift_weight, back_weight):
    lifted = jnp.dot(lift_weight, state.astype(jnp.bfloat16), preferred_element_type=jnp.float32)
    squared = (lifted * lifted).astype(jnp.bfloat16)
    source = jnp.dot(back_weight, squared, preferred_element_type=jnp.float32)
    return state + coupling * source


def shards(wave_energy, courant, sea_mask, lift_weight, back_weight):
    devices_count = lax.axis_size("cell")
    device_rank = lax.axis_index("cell")
    groups, all_cells = wave_energy.shape
    tile_cells = all_cells // devices_count
    sea_field = sea_mask.astype(jnp.float32)
    first_speeds = lax.dynamic_slice_in_dim(courant, device_rank * groups, groups)[:, None]
    local = jnp.pad(wave_energy, ((0, 0), (4, 4)))
    padded_sea = jnp.pad(sea_field, 4)
    local = substep(local, padded_sea, first_speeds)
    local = substep(local, padded_sea[2:-2], first_speeds)
    tile_state = lax.all_to_all(local, "cell", split_axis=1, concat_axis=0, tiled=True)
    speeds = courant[:, None]
    local_sea = lax.dynamic_slice_in_dim(padded_sea, device_rank * tile_cells, tile_cells + 8)
    tile_state = fourwave(tile_state, lift_weight, back_weight)
    for repeat in range(STEPS - 1):
        extended = with_halo(tile_state, (("cell", 1),), 4)
        extended = substep(extended, local_sea, speeds)
        tile_state = substep(extended, local_sea[2:-2], speeds)
        tile_state = fourwave(tile_state, lift_weight, back_weight)
    return lax.all_to_all(tile_state, "cell", split_axis=0, concat_axis=1, tiled=True)


def solution(mesh):
    placed = (P(("member", "cell"), None), P(), P(), P(), P())
    return jax.shard_map(
        shards, mesh=mesh, in_specs=placed, out_specs=P(("member", "cell"), None), check_vma=False
    )
```

```python
import functools

import jax
import jax.numpy as jnp
from jax import lax
from jax.experimental import pallas as pl
from jax.experimental.pallas import tpu as pltpu
from jax.sharding import PartitionSpec as P

STEPS = 2
LANES = 128
MESH = pl.DeviceIdType.MESH

coupling = 0.25


def minmod(first_term, second_term):
    low = jnp.minimum(first_term, second_term)
    high = jnp.maximum(first_term, second_term)
    return jnp.maximum(low, 0.0) + jnp.minimum(high, 0.0)


def step_pair(spectra, open_faces, speeds):
    width = spectra.shape[1]
    forward = jnp.maximum(speeds, 0.0)
    backward = jnp.minimum(speeds, 0.0)
    forward_half = 0.5 * (1.0 - forward)
    backward_half = 0.5 * (1.0 + backward)
    for _ in range(2):
        ahead = pltpu.roll(spectra, width - 1, 1) - spectra
        slopes = minmod(ahead, pltpu.roll(ahead, 1, 1))
        from_left = forward * (spectra + forward_half * slopes)
        from_right = backward * (spectra - backward_half * slopes)
        fluxes = (from_left + pltpu.roll(from_right, width - 1, 1)) * open_faces
        spectra = spectra - (fluxes - pltpu.roll(fluxes, 1, 1))
    return spectra


def kernel(
    n, u_ref, speed_ref, sea_ref, lift_hbm, back_hbm, out_ref,
    sent, got, state, rounded, squared, result, sea, lift, back,
    load_sem, own_sem, send_one, recv_one, send_two, recv_two,
):
    me = lax.axis_index("cell")
    depth = u_ref.shape[0]
    packs = depth // 8
    modes, comps = lift.shape

    barrier = pltpu.get_barrier_semaphore()

    def greet(k, _):
        other = lax.rem(me + k, n)
        pl.semaphore_signal(barrier, inc=1, device_id={"cell": other}, device_id_type=MESH)
        return 0

    lax.fori_loop(1, n, greet, 0)
    load_lift = pltpu.make_async_copy(lift_hbm, lift, load_sem.at[0])
    load_back = pltpu.make_async_copy(back_hbm, back, load_sem.at[1])
    load_lift.start()
    load_back.start()

    cells = n * LANES
    sea_row = sea_ref[...].astype(jnp.float32)
    sea[:, :cells] = jnp.broadcast_to(sea_row, (8, cells))
    sea[:, cells:] = jnp.zeros((8, LANES), jnp.float32)
    all_sea = sea[...]
    all_open = all_sea * pltpu.roll(all_sea, cells + LANES - 1, 1)
    lane = lax.broadcasted_iota(jnp.int32, (8, LANES), 1)

    for g in range(packs):
        rows = pl.ds(g * 8, 8)
        own_rows = pl.ds(pl.multiple_of(me * depth + g * 8, 8), 8)
        block = jnp.concatenate([u_ref[rows, :], jnp.zeros((8, LANES), jnp.float32)], axis=1)
        block = step_pair(block, all_open, speed_ref[own_rows, :])
        tiles = [block[:, t * LANES : (t + 1) * LANES] for t in range(n + 1)]
        for t in range(n):
            sent[t, rows, :] = tiles[t]
            edge = jnp.where(lane < 64, tiles[t + 1], tiles[t - 1])
            if g:
                edge = pltpu.roll(edge, 8 * g, 1)
                mine = (lane >= 8 * g - 4) & (lane < 8 * g + 4)
                edge = jnp.where(mine, edge, sent[t, depth : depth + 8, :])
            sent[t, depth : depth + 8, :] = edge

    def first(dest, source):
        return pltpu.make_async_remote_copy(
            src_ref=sent.at[dest], dst_ref=got.at[source],
            send_sem=send_one.at[dest], recv_sem=recv_one.at[source],
            device_id={"cell": dest}, device_id_type=MESH,
        )

    pl.semaphore_wait(barrier, n - 1)

    def push(k, _):
        first(lax.rem(me + k, n), me).start()
        return 0

    lax.fori_loop(1, n, push, 0)

    main_sea = sea[:, pl.ds(pl.multiple_of(me * LANES, LANES), LANES)]
    next_sea = sea[:, pl.ds(pl.multiple_of((me + 1) * LANES, LANES), LANES)]
    last_tile = lax.rem(me + n, n + 1)
    last_sea = sea[:, pl.ds(pl.multiple_of(last_tile * LANES, LANES), LANES)]
    side_sea = jnp.where(lane < 4, next_sea, jnp.where(lane >= LANES - 4, last_sea, 0.0))
    near_sea = jnp.concatenate([main_sea, side_sea], axis=1)
    near_open = (near_sea * pltpu.roll(near_sea, 2 * LANES - 1, 1))[0:1, :]

    def unpack(source, block):
        halo = (lane < 4) | (lane >= LANES - 4)
        edge = block[depth : depth + 8, :]
        for g in range(packs):
            rows = pl.ds(pl.multiple_of(source * depth + g * 8, 8), 8)
            state[rows, 0:LANES] = block[g * 8 : g * 8 + 8, :]
            turned = pltpu.roll(edge, LANES - 8 * g, 1) if g else edge
            state[rows, LANES:] = jnp.where(halo, turned, 0.0)

    unpack(me, sent[me])

    def pull(k, _):
        source = lax.rem(me + n - k, n)
        first(source, source).wait_recv()
        unpack(source, got[source])
        return 0

    lax.fori_loop(1, n, pull, 0)

    wide = 64

    def narrow(i, _):
        rows = pl.ds(pl.multiple_of(i * wide, wide), wide)
        rounded[rows, :] = state[rows, :].astype(jnp.bfloat16)
        return 0

    lax.fori_loop(0, comps // wide, narrow, 0)

    mode_part, comp_part = modes // 4, comps // 4

    def lifting(width):
        def body(i, _):
            rows = pl.ds(pl.multiple_of(i * mode_part, mode_part), mode_part)
            lifted = jnp.dot(
                lift[rows, :], rounded[:, :width], preferred_element_type=jnp.float32
            )
            squared[rows, :width] = (lifted * lifted).astype(jnp.bfloat16)
            return 0

        lax.fori_loop(0, 4, body, 0)

    load_lift.wait()
    lifting(2 * LANES)
    load_back.wait()

    def source_one(i, _):
        rows = pl.ds(pl.multiple_of(i * comp_part, comp_part), comp_part)
        source = jnp.dot(back[rows, :], squared[...], preferred_element_type=jnp.float32)
        state[rows, :] = state[rows, :] + coupling * source
        return 0

    lax.fori_loop(0, 4, source_one, 0)

    def propagate(i, _):
        rows = pl.ds(pl.multiple_of(i * wide, wide), wide)
        block = step_pair(state[rows, :], near_open, speed_ref[rows, :])[:, :LANES]
        state[rows, 0:LANES] = block
        rounded[rows, 0:LANES] = block.astype(jnp.bfloat16)
        return 0

    lax.fori_loop(0, comps // wide, propagate, 0)
    lifting(LANES)

    def place(source):
        return out_ref.at[:, pl.ds(pl.multiple_of(source * LANES, LANES), LANES)]

    def second(dest, source):
        return pltpu.make_async_remote_copy(
            src_ref=result.at[dest], dst_ref=place(source),
            send_sem=send_two.at[dest], recv_sem=recv_two.at[source],
            device_id={"cell": dest}, device_id_type=MESH,
        )

    own = pltpu.make_async_copy(result.at[me], place(me), own_sem)
    part = n // 4

    def source_two(i, _):
        rows = pl.ds(pl.multiple_of(i * comp_part, comp_part), comp_part)
        source = jnp.dot(
            back[rows, :], squared[:, :LANES], preferred_element_type=jnp.float32
        )
        total = state[rows, 0:LANES] + coupling * source
        result[pl.ds(i * part, part)] = total.reshape(part, depth, LANES)

        def send(j, _):
            dest = i * part + j

            @pl.when(dest != me)
            def _():
                second(dest, me).start()

            return 0

        lax.fori_loop(0, part, send, 0)
        return 0

    lax.fori_loop(0, 4, source_two, 0)
    own.start()

    def finish(k, _):
        dest = lax.rem(me + k, n)
        source = lax.rem(me + n - k, n)
        first(dest, me).wait_send()
        second(dest, me).wait_send()
        second(source, source).wait_recv()
        return 0

    lax.fori_loop(1, n, finish, 0)
    own.wait()


def shards(wave_energy, courant, sea_mask, lift_weight, back_weight):
    n = lax.axis_size("cell")
    groups, cells = wave_energy.shape
    modes = lift_weight.shape[0]
    depth = -(-groups // 8) * 8
    extra = depth - groups
    if extra:
        wave_energy = jnp.pad(wave_energy, ((0, extra), (0, 0)))
        courant = jnp.pad(courant.reshape(n, groups), ((0, 0), (0, extra))).reshape(-1)
        lift_weight = jnp.pad(
            lift_weight.reshape(modes, n, groups), ((0, 0), (0, 0), (0, extra))
        ).reshape(modes, n * depth)
        back_weight = jnp.pad(
            back_weight.reshape(n, groups, modes), ((0, 0), (0, extra), (0, 0))
        ).reshape(n * depth, modes)
    comps = n * depth
    vmem = pl.BlockSpec(memory_space=pltpu.VMEM)
    anywhere = pl.BlockSpec(memory_space=pl.ANY)
    out = pl.pallas_call(
        functools.partial(kernel, n),
        out_shape=jax.ShapeDtypeStruct((depth, cells), jnp.float32),
        in_specs=[vmem, vmem, vmem, anywhere, anywhere],
        out_specs=anywhere,
        scratch_shapes=[
            pltpu.VMEM((n, depth + 8, LANES), jnp.float32),
            pltpu.VMEM((n, depth + 8, LANES), jnp.float32),
            pltpu.VMEM((comps, 2 * LANES), jnp.float32),
            pltpu.VMEM((comps, 2 * LANES), jnp.bfloat16),
            pltpu.VMEM((modes, 2 * LANES), jnp.bfloat16),
            pltpu.VMEM((n, depth, LANES), jnp.float32),
            pltpu.VMEM((8, cells + LANES), jnp.float32),
            pltpu.VMEM((modes, comps), jnp.bfloat16),
            pltpu.VMEM((comps, modes), jnp.bfloat16),
            pltpu.SemaphoreType.DMA((2,)),
            pltpu.SemaphoreType.DMA,
            pltpu.SemaphoreType.DMA((n,)),
            pltpu.SemaphoreType.DMA((n,)),
            pltpu.SemaphoreType.DMA((n,)),
            pltpu.SemaphoreType.DMA((n,)),
        ],
        compiler_params=pltpu.CompilerParams(collective_id=0, has_side_effects=True),
    )(wave_energy, courant[:, None], sea_mask[None, :], lift_weight, back_weight)
    return out[:groups]


def solution(mesh):
    placed = (P(("member", "cell"), None), P(), P(), P(), P())
    return jax.shard_map(
        shards, mesh=mesh, in_specs=placed, out_specs=P(("member", "cell"), None), check_vma=False
    )
```

```python
import functools

import jax
import jax.numpy as jnp
from jax import lax
from jax.experimental import pallas as pl
from jax.experimental.pallas import tpu as pltpu
from jax.sharding import PartitionSpec as P

STEPS = 2
LANES = 128
MESH = pl.DeviceIdType.MESH

coupling = 0.25


def minmod(first_term, second_term):
    low = jnp.minimum(first_term, second_term)
    high = jnp.maximum(first_term, second_term)
    return jnp.maximum(low, 0.0) + jnp.minimum(high, 0.0)


def step_pair(spectra, open_faces, speeds):
    width = spectra.shape[1]
    eastward = speeds >= 0.0
    weight = jnp.where(eastward, 0.5 * (1.0 - speeds), -0.5 * (1.0 + speeds))
    open_before = pltpu.roll(open_faces, 1, 1)
    for _ in range(2):
        ahead = pltpu.roll(spectra, width - 1, 1) - spectra
        behind = spectra - pltpu.roll(spectra, 1, 1)
        carried = speeds * (spectra + weight * minmod(ahead, behind))
        after = jnp.where(eastward, carried, pltpu.roll(carried, width - 1, 1))
        before = jnp.where(eastward, pltpu.roll(carried, 1, 1), carried)
        spectra = spectra - (after * open_faces - before * open_before)
    return spectra


def kernel(
    n, u_ref, speed_ref, sea_ref, lift_hbm, back_hbm, out_ref,
    sent, got, state, rounded, squared, result, sea, speeds, lift, back,
    load_sem, own_sem, send_one, recv_one, send_two, recv_two,
):
    me = lax.axis_index("cell")
    depth = u_ref.shape[0]
    packs = depth // 8
    modes, comps = lift.shape

    barrier = pltpu.get_barrier_semaphore()

    def greet(k, _):
        other = lax.rem(me + k, n)
        pl.semaphore_signal(barrier, inc=1, device_id={"cell": other}, device_id_type=MESH)
        return 0

    lax.fori_loop(1, n, greet, 0)
    load_lift = pltpu.make_async_copy(lift_hbm, lift, load_sem.at[0])
    load_back = pltpu.make_async_copy(back_hbm, back, load_sem.at[1])
    load_lift.start()
    load_back.start()

    cells = n * LANES
    sea_row = sea_ref[...].astype(jnp.float32)
    sea[:, :cells] = jnp.broadcast_to(sea_row, (8, cells))
    sea[:, cells:] = jnp.zeros((8, LANES), jnp.float32)
    all_sea = sea[...]
    all_open = all_sea * pltpu.roll(all_sea, cells + LANES - 1, 1)
    lane = lax.broadcasted_iota(jnp.int32, (8, LANES), 1)

    for r in range(speed_ref.shape[0]):
        row = jnp.broadcast_to(speed_ref[r : r + 1, :], (LANES, LANES))
        speeds[r * LANES : (r + 1) * LANES, :] = jnp.transpose(row)

    for g in range(packs):
        rows = pl.ds(g * 8, 8)
        own_rows = pl.ds(pl.multiple_of(me * depth + g * 8, 8), 8)
        block = jnp.concatenate([u_ref[rows, :], jnp.zeros((8, LANES), jnp.float32)], axis=1)
        own_speeds = jnp.concatenate([speeds[own_rows, :]] * (n + 1), axis=1)
        block = step_pair(block, all_open, own_speeds)
        tiles = [block[:, t * LANES : (t + 1) * LANES] for t in range(n + 1)]
        for t in range(n):
            sent[t, rows, :] = tiles[t]
            edge = jnp.where(lane < 64, tiles[t + 1], tiles[t - 1])
            if g:
                edge = pltpu.roll(edge, 8 * g, 1)
                mine = (lane >= 8 * g - 4) & (lane < 8 * g + 4)
                edge = jnp.where(mine, edge, sent[t, depth : depth + 8, :])
            sent[t, depth : depth + 8, :] = edge

    def first(dest, source):
        return pltpu.make_async_remote_copy(
            src_ref=sent.at[dest], dst_ref=got.at[source],
            send_sem=send_one.at[dest], recv_sem=recv_one.at[source],
            device_id={"cell": dest}, device_id_type=MESH,
        )

    pl.semaphore_wait(barrier, n - 1)

    def push(k, _):
        first(lax.rem(me + k, n), me).start()
        return 0

    lax.fori_loop(1, n, push, 0)

    main_sea = sea[:, pl.ds(pl.multiple_of(me * LANES, LANES), LANES)]
    next_sea = sea[:, pl.ds(pl.multiple_of((me + 1) * LANES, LANES), LANES)]
    last_tile = lax.rem(me + n, n + 1)
    last_sea = sea[:, pl.ds(pl.multiple_of(last_tile * LANES, LANES), LANES)]
    side_sea = jnp.where(lane < 4, next_sea, jnp.where(lane >= LANES - 4, last_sea, 0.0))
    near_sea = jnp.concatenate([main_sea, side_sea], axis=1)
    near_open = (near_sea * pltpu.roll(near_sea, 2 * LANES - 1, 1))[0:1, :]

    def unpack(source, block):
        halo = (lane < 4) | (lane >= LANES - 4)
        edge = block[depth : depth + 8, :]
        for g in range(packs):
            rows = pl.ds(pl.multiple_of(source * depth + g * 8, 8), 8)
            state[rows, 0:LANES] = block[g * 8 : g * 8 + 8, :]
            turned = pltpu.roll(edge, LANES - 8 * g, 1) if g else edge
            state[rows, LANES:] = jnp.where(halo, turned, 0.0)

    unpack(me, sent[me])

    def pull(k, _):
        source = lax.rem(me + n - k, n)
        first(source, source).wait_recv()
        unpack(source, got[source])
        return 0

    lax.fori_loop(1, n, pull, 0)

    wide = 64

    def narrow(i, _):
        rows = pl.ds(pl.multiple_of(i * wide, wide), wide)
        rounded[rows, :] = state[rows, :].astype(jnp.bfloat16)
        return 0

    lax.fori_loop(0, comps // wide, narrow, 0)

    mode_part, comp_part = modes // 4, comps // 4

    def lifting(width):
        def body(i, _):
            rows = pl.ds(pl.multiple_of(i * mode_part, mode_part), mode_part)
            lifted = jnp.dot(
                lift[rows, :], rounded[:, :width], preferred_element_type=jnp.float32
            )
            squared[rows, :width] = (lifted * lifted).astype(jnp.bfloat16)
            return 0

        lax.fori_loop(0, 4, body, 0)

    load_lift.wait()
    lifting(2 * LANES)
    load_back.wait()

    def source_one(i, _):
        rows = pl.ds(pl.multiple_of(i * comp_part, comp_part), comp_part)
        source = jnp.dot(back[rows, :], squared[...], preferred_element_type=jnp.float32)
        state[rows, :] = state[rows, :] + coupling * source
        return 0

    lax.fori_loop(0, 4, source_one, 0)

    slab, piece = 128, 32
    near_open = jnp.broadcast_to(near_open, (piece, 2 * LANES))

    def propagate(i, _):
        spans = [
            pl.ds(pl.multiple_of(i * slab + j * piece, piece), piece) for j in range(slab // piece)
        ]
        before = [state[rows, :] for rows in spans]
        after = [
            step_pair(block, near_open, jnp.concatenate([speeds[rows, :]] * 2, axis=1))
            for rows, block in zip(spans, before)
        ]
        for rows, block in zip(spans, after):
            state[rows, 0:LANES] = block[:, :LANES]
            rounded[rows, 0:LANES] = block[:, :LANES].astype(jnp.bfloat16)
        return 0

    lax.fori_loop(0, comps // slab, propagate, 0)
    lifting(LANES)

    def place(source):
        return out_ref.at[source]

    def second(dest, source):
        return pltpu.make_async_remote_copy(
            src_ref=result.at[dest], dst_ref=place(source),
            send_sem=send_two.at[dest], recv_sem=recv_two.at[source],
            device_id={"cell": dest}, device_id_type=MESH,
        )

    own = pltpu.make_async_copy(result.at[me], place(me), own_sem)
    part = n // 4

    def source_two(i, _):
        rows = pl.ds(pl.multiple_of(i * comp_part, comp_part), comp_part)
        source = jnp.dot(
            back[rows, :], squared[:, :LANES], preferred_element_type=jnp.float32
        )
        total = state[rows, 0:LANES] + coupling * source
        result[pl.ds(i * part, part)] = total.reshape(part, depth, LANES)

        def send(j, _):
            dest = i * part + j

            @pl.when(dest != me)
            def _():
                second(dest, me).start()

            return 0

        lax.fori_loop(0, part, send, 0)
        return 0

    lax.fori_loop(0, 4, source_two, 0)
    own.start()

    def finish(k, _):
        dest = lax.rem(me + k, n)
        source = lax.rem(me + n - k, n)
        first(dest, me).wait_send()
        second(dest, me).wait_send()
        second(source, source).wait_recv()
        return 0

    lax.fori_loop(1, n, finish, 0)
    own.wait()


def shards(wave_energy, courant, sea_mask, lift_weight, back_weight):
    n = lax.axis_size("cell")
    groups, cells = wave_energy.shape
    modes = lift_weight.shape[0]
    depth = -(-groups // 8) * 8
    extra = depth - groups
    if extra:
        wave_energy = jnp.pad(wave_energy, ((0, extra), (0, 0)))
        courant = jnp.pad(courant.reshape(n, groups), ((0, 0), (0, extra))).reshape(-1)
        lift_weight = jnp.pad(
            lift_weight.reshape(modes, n, groups), ((0, 0), (0, 0), (0, extra))
        ).reshape(modes, n * depth)
        back_weight = jnp.pad(
            back_weight.reshape(n, groups, modes), ((0, 0), (0, extra), (0, 0))
        ).reshape(n * depth, modes)
    comps = n * depth
    speed_rows = jnp.pad(courant, (0, -comps % LANES)).reshape(-1, LANES)
    vmem = pl.BlockSpec(memory_space=pltpu.VMEM)
    anywhere = pl.BlockSpec(memory_space=pl.ANY)
    out = pl.pallas_call(
        functools.partial(kernel, n),
        out_shape=jax.ShapeDtypeStruct((n, depth, cells // n), jnp.float32),
        in_specs=[vmem, vmem, vmem, anywhere, anywhere],
        out_specs=anywhere,
        scratch_shapes=[
            pltpu.VMEM((n, depth + 8, LANES), jnp.float32),
            pltpu.VMEM((n, depth + 8, LANES), jnp.float32),
            pltpu.VMEM((comps, 2 * LANES), jnp.float32),
            pltpu.VMEM((comps, 2 * LANES), jnp.bfloat16),
            pltpu.VMEM((modes, 2 * LANES), jnp.bfloat16),
            pltpu.VMEM((n, depth, LANES), jnp.float32),
            pltpu.VMEM((8, cells + LANES), jnp.float32),
            pltpu.VMEM((speed_rows.size, LANES), jnp.float32),
            pltpu.VMEM((modes, comps), jnp.bfloat16),
            pltpu.VMEM((comps, modes), jnp.bfloat16),
            pltpu.SemaphoreType.DMA((2,)),
            pltpu.SemaphoreType.DMA,
            pltpu.SemaphoreType.DMA((n,)),
            pltpu.SemaphoreType.DMA((n,)),
            pltpu.SemaphoreType.DMA((n,)),
            pltpu.SemaphoreType.DMA((n,)),
        ],
        compiler_params=pltpu.CompilerParams(collective_id=0, has_side_effects=True),
    )(wave_energy, speed_rows, sea_mask[None, :], lift_weight, back_weight)
    return out.transpose(1, 0, 2).reshape(depth, cells)[:groups]


def solution(mesh):
    placed = (P(("member", "cell"), None), P(), P(), P(), P())
    return jax.shard_map(
        shards, mesh=mesh, in_specs=placed, out_specs=P(("member", "cell"), None), check_vma=False
    )
```

```python
import functools

import jax
import jax.numpy as jnp
from jax import lax
from jax.experimental import pallas as pl
from jax.experimental.pallas import tpu as pltpu
from jax.sharding import PartitionSpec as P

STEPS = 2
LANES = 128
MESH = pl.DeviceIdType.MESH

coupling = 0.25


def minmod(first_term, second_term):
    low = jnp.minimum(first_term, second_term)
    high = jnp.maximum(first_term, second_term)
    return jnp.maximum(low, 0.0) + jnp.minimum(high, 0.0)


def step_pair(spectra, open_faces, speeds):
    width = spectra.shape[1]
    eastward = speeds >= 0.0
    weight = jnp.where(eastward, 0.5 * (1.0 - speeds), -0.5 * (1.0 + speeds))
    open_before = pltpu.roll(open_faces, 1, 1)
    for _ in range(2):
        ahead = pltpu.roll(spectra, width - 1, 1) - spectra
        behind = spectra - pltpu.roll(spectra, 1, 1)
        carried = speeds * (spectra + weight * minmod(ahead, behind))
        after = jnp.where(eastward, carried, pltpu.roll(carried, width - 1, 1))
        before = jnp.where(eastward, pltpu.roll(carried, 1, 1), carried)
        spectra = spectra - (after * open_faces - before * open_before)
    return spectra


def kernel(
    n, u_ref, speed_ref, sea_ref, lift_hbm, back_hbm, out_ref,
    sent, got, state, rounded, squared, result, sea, speeds, lift, back,
    load_sem, own_sem, send_one, recv_one, send_two, recv_two,
):
    me = lax.axis_index("cell")
    depth = u_ref.shape[0]
    packs = depth // 8
    modes, comps = lift.shape

    barrier = pltpu.get_barrier_semaphore()

    def greet(k, _):
        other = lax.rem(me + k, n)
        pl.semaphore_signal(barrier, inc=1, device_id={"cell": other}, device_id_type=MESH)
        return 0

    lax.fori_loop(1, n, greet, 0)
    load_lift = pltpu.make_async_copy(lift_hbm, lift, load_sem.at[0])
    load_back = pltpu.make_async_copy(back_hbm, back, load_sem.at[1])
    load_lift.start()
    load_back.start()

    cells = n * LANES
    sea_row = sea_ref[...].astype(jnp.float32)
    sea[:, :cells] = jnp.broadcast_to(sea_row, (8, cells))
    sea[:, cells:] = jnp.zeros((8, LANES), jnp.float32)
    all_sea = sea[...]
    all_open = all_sea * pltpu.roll(all_sea, cells + LANES - 1, 1)
    lane = lax.broadcasted_iota(jnp.int32, (8, LANES), 1)

    for r in range(speed_ref.shape[0]):
        row = jnp.broadcast_to(speed_ref[r : r + 1, :], (LANES, LANES))
        speeds[r * LANES : (r + 1) * LANES, :] = jnp.transpose(row)

    for g in range(packs):
        rows = pl.ds(g * 8, 8)
        own_rows = pl.ds(pl.multiple_of(me * depth + g * 8, 8), 8)
        block = jnp.concatenate([u_ref[rows, :], jnp.zeros((8, LANES), jnp.float32)], axis=1)
        own_speeds = jnp.concatenate([speeds[own_rows, :]] * (n + 1), axis=1)
        block = step_pair(block, all_open, own_speeds)
        tiles = [block[:, t * LANES : (t + 1) * LANES] for t in range(n + 1)]
        for t in range(n):
            sent[t, rows, :] = tiles[t]
            edge = jnp.where(lane < 64, tiles[t + 1], tiles[t - 1])
            if g:
                edge = pltpu.roll(edge, 8 * g, 1)
                mine = (lane >= 8 * g - 4) & (lane < 8 * g + 4)
                edge = jnp.where(mine, edge, sent[t, depth : depth + 8, :])
            sent[t, depth : depth + 8, :] = edge

    def first(dest, source):
        return pltpu.make_async_remote_copy(
            src_ref=sent.at[dest], dst_ref=got.at[source],
            send_sem=send_one.at[dest], recv_sem=recv_one.at[source],
            device_id={"cell": dest}, device_id_type=MESH,
        )

    pl.semaphore_wait(barrier, n - 1)

    def push(k, _):
        first(lax.rem(me + n - k, n), me).start()
        return 0

    lax.fori_loop(1, n, push, 0)

    main_sea = sea[:, pl.ds(pl.multiple_of(me * LANES, LANES), LANES)]
    next_sea = sea[:, pl.ds(pl.multiple_of((me + 1) * LANES, LANES), LANES)]
    last_tile = lax.rem(me + n, n + 1)
    last_sea = sea[:, pl.ds(pl.multiple_of(last_tile * LANES, LANES), LANES)]
    side_sea = jnp.where(lane < 4, next_sea, jnp.where(lane >= LANES - 4, last_sea, 0.0))
    near_sea = jnp.concatenate([main_sea, side_sea], axis=1)
    near_open = (near_sea * pltpu.roll(near_sea, 2 * LANES - 1, 1))[0:1, :]

    def unpack(source, block):
        halo = (lane < 4) | (lane >= LANES - 4)
        edge = block[depth : depth + 8, :]
        for g in range(packs):
            rows = pl.ds(pl.multiple_of(source * depth + g * 8, 8), 8)
            state[rows, 0:LANES] = block[g * 8 : g * 8 + 8, :]
            turned = pltpu.roll(edge, LANES - 8 * g, 1) if g else edge
            state[rows, LANES:] = jnp.where(halo, turned, 0.0)

    unpack(me, sent[me])

    def pull(k, _):
        source = lax.rem(me + k, n)
        first(source, source).wait_recv()
        unpack(source, got[source])
        return 0

    lax.fori_loop(1, n, pull, 0)

    wide = 64

    def narrow(i, _):
        rows = pl.ds(pl.multiple_of(i * wide, wide), wide)
        rounded[rows, :] = state[rows, :].astype(jnp.bfloat16)
        return 0

    lax.fori_loop(0, comps // wide, narrow, 0)

    mode_part, comp_part = modes // 4, comps // 4

    def lifting(width):
        def body(i, _):
            rows = pl.ds(pl.multiple_of(i * mode_part, mode_part), mode_part)
            lifted = jnp.dot(
                lift[rows, :], rounded[:, :width], preferred_element_type=jnp.float32
            )
            squared[rows, :width] = (lifted * lifted).astype(jnp.bfloat16)
            return 0

        lax.fori_loop(0, 4, body, 0)

    load_lift.wait()
    lifting(2 * LANES)
    load_back.wait()

    def source_one(i, _):
        rows = pl.ds(pl.multiple_of(i * comp_part, comp_part), comp_part)
        source = jnp.dot(back[rows, :], squared[...], preferred_element_type=jnp.float32)
        state[rows, :] = state[rows, :] + coupling * source
        return 0

    lax.fori_loop(0, 4, source_one, 0)

    slab, piece = 128, 32
    near_open = jnp.broadcast_to(near_open, (piece, 2 * LANES))

    def propagate(i, _):
        spans = [
            pl.ds(pl.multiple_of(i * slab + j * piece, piece), piece) for j in range(slab // piece)
        ]
        before = [state[rows, :] for rows in spans]
        after = [
            step_pair(block, near_open, jnp.concatenate([speeds[rows, :]] * 2, axis=1))
            for rows, block in zip(spans, before)
        ]
        for rows, block in zip(spans, after):
            state[rows, 0:LANES] = block[:, :LANES]
            rounded[rows, 0:LANES] = block[:, :LANES].astype(jnp.bfloat16)
        return 0

    lax.fori_loop(0, comps // slab, propagate, 0)
    lifting(LANES)

    def place(source):
        return out_ref.at[source]

    def second(dest, source):
        return pltpu.make_async_remote_copy(
            src_ref=result.at[dest], dst_ref=place(source),
            send_sem=send_two.at[dest], recv_sem=recv_two.at[source],
            device_id={"cell": dest}, device_id_type=MESH,
        )

    own = pltpu.make_async_copy(result.at[me], place(me), own_sem)
    part = n // 4

    def source_two(step, _):
        i = lax.rem(me // part + 1 + step, 4)
        rows = pl.ds(pl.multiple_of(i * comp_part, comp_part), comp_part)
        source = jnp.dot(
            back[rows, :], squared[:, :LANES], preferred_element_type=jnp.float32
        )
        total = state[rows, 0:LANES] + coupling * source
        result[pl.ds(i * part, part)] = total.reshape(part, depth, LANES)

        def send(j, _):
            dest = i * part + j

            @pl.when(dest != me)
            def _():
                second(dest, me).start()

            return 0

        lax.fori_loop(0, part, send, 0)
        return 0

    lax.fori_loop(0, 4, source_two, 0)
    own.start()

    def finish(k, _):
        dest = lax.rem(me + k, n)
        source = lax.rem(me + n - k, n)
        first(dest, me).wait_send()
        second(dest, me).wait_send()
        second(source, source).wait_recv()
        return 0

    lax.fori_loop(1, n, finish, 0)
    own.wait()


def shards(wave_energy, courant, sea_mask, lift_weight, back_weight):
    n = lax.axis_size("cell")
    groups, cells = wave_energy.shape
    modes = lift_weight.shape[0]
    depth = -(-groups // 8) * 8
    extra = depth - groups
    if extra:
        wave_energy = jnp.pad(wave_energy, ((0, extra), (0, 0)))
        courant = jnp.pad(courant.reshape(n, groups), ((0, 0), (0, extra))).reshape(-1)
        lift_weight = jnp.pad(
            lift_weight.reshape(modes, n, groups), ((0, 0), (0, 0), (0, extra))
        ).reshape(modes, n * depth)
        back_weight = jnp.pad(
            back_weight.reshape(n, groups, modes), ((0, 0), (0, extra), (0, 0))
        ).reshape(n * depth, modes)
    comps = n * depth
    speed_rows = jnp.pad(courant, (0, -comps % LANES)).reshape(-1, LANES)
    vmem = pl.BlockSpec(memory_space=pltpu.VMEM)
    anywhere = pl.BlockSpec(memory_space=pl.ANY)
    out = pl.pallas_call(
        functools.partial(kernel, n),
        out_shape=jax.ShapeDtypeStruct((n, depth, cells // n), jnp.float32),
        in_specs=[vmem, vmem, vmem, anywhere, anywhere],
        out_specs=anywhere,
        scratch_shapes=[
            pltpu.VMEM((n, depth + 8, LANES), jnp.float32),
            pltpu.VMEM((n, depth + 8, LANES), jnp.float32),
            pltpu.VMEM((comps, 2 * LANES), jnp.float32),
            pltpu.VMEM((comps, 2 * LANES), jnp.bfloat16),
            pltpu.VMEM((modes, 2 * LANES), jnp.bfloat16),
            pltpu.VMEM((n, depth, LANES), jnp.float32),
            pltpu.VMEM((8, cells + LANES), jnp.float32),
            pltpu.VMEM((speed_rows.size, LANES), jnp.float32),
            pltpu.VMEM((modes, comps), jnp.bfloat16),
            pltpu.VMEM((comps, modes), jnp.bfloat16),
            pltpu.SemaphoreType.DMA((2,)),
            pltpu.SemaphoreType.DMA,
            pltpu.SemaphoreType.DMA((n,)),
            pltpu.SemaphoreType.DMA((n,)),
            pltpu.SemaphoreType.DMA((n,)),
            pltpu.SemaphoreType.DMA((n,)),
        ],
        compiler_params=pltpu.CompilerParams(collective_id=0, has_side_effects=True),
    )(wave_energy, speed_rows, sea_mask[None, :], lift_weight, back_weight)
    return out.transpose(1, 0, 2).reshape(depth, cells)[:groups]


def solution(mesh):
    placed = (P(("member", "cell"), None), P(), P(), P(), P())
    return jax.shard_map(
        shards, mesh=mesh, in_specs=placed, out_specs=P(("member", "cell"), None), check_vma=False
    )
```

```python
import functools

import jax
import jax.numpy as jnp
from jax import lax
from jax.experimental import pallas as pl
from jax.experimental.pallas import tpu as pltpu
from jax.sharding import PartitionSpec as P

STEPS = 2
LANES = 128
MESH = pl.DeviceIdType.MESH

coupling = 0.25


def minmod(first_term, second_term):
    low = jnp.minimum(first_term, second_term)
    high = jnp.maximum(first_term, second_term)
    return jnp.maximum(low, 0.0) + jnp.minimum(high, 0.0)


def step_pair(spectra, open_faces, speeds):
    width = spectra.shape[1]
    eastward = speeds >= 0.0
    weight = jnp.where(eastward, 0.5 * (1.0 - speeds), -0.5 * (1.0 + speeds))
    open_before = pltpu.roll(open_faces, 1, 1)
    for _ in range(2):
        ahead = pltpu.roll(spectra, width - 1, 1) - spectra
        behind = spectra - pltpu.roll(spectra, 1, 1)
        carried = speeds * (spectra + weight * minmod(ahead, behind))
        after = jnp.where(eastward, carried, pltpu.roll(carried, width - 1, 1))
        before = jnp.where(eastward, pltpu.roll(carried, 1, 1), carried)
        spectra = spectra - (after * open_faces - before * open_before)
    return spectra


def kernel(
    n, u_ref, speed_ref, sea_ref, lift_hbm, back_hbm, out_ref,
    sent, got, state, rounded, squared, result, sea, speeds, lift, back,
    load_sem, own_sem, send_one, recv_one, send_two, recv_two,
):
    me = lax.axis_index("cell")
    depth = u_ref.shape[0]
    packs = depth // 8
    modes, comps = lift.shape

    barrier = pltpu.get_barrier_semaphore()

    def greet(k, _):
        other = lax.rem(me + k, n)
        pl.semaphore_signal(barrier, inc=1, device_id={"cell": other}, device_id_type=MESH)
        return 0

    lax.fori_loop(1, n, greet, 0)
    load_lift = pltpu.make_async_copy(lift_hbm, lift, load_sem.at[0])
    load_back = pltpu.make_async_copy(back_hbm, back, load_sem.at[1])
    load_lift.start()
    load_back.start()

    cells = n * LANES
    sea_row = sea_ref[...].astype(jnp.float32)
    sea[:, :cells] = jnp.broadcast_to(sea_row, (8, cells))
    sea[:, cells:] = jnp.zeros((8, LANES), jnp.float32)
    all_sea = sea[...]
    all_open = all_sea * pltpu.roll(all_sea, cells + LANES - 1, 1)
    lane = lax.broadcasted_iota(jnp.int32, (8, LANES), 1)

    for r in range(speed_ref.shape[0]):
        row = jnp.broadcast_to(speed_ref[r : r + 1, :], (LANES, LANES))
        speeds[r * LANES : (r + 1) * LANES, :] = jnp.transpose(row)

    for g in range(packs):
        rows = pl.ds(g * 8, 8)
        own_rows = pl.ds(pl.multiple_of(me * depth + g * 8, 8), 8)
        block = jnp.concatenate([u_ref[rows, :], jnp.zeros((8, LANES), jnp.float32)], axis=1)
        own_speeds = jnp.concatenate([speeds[own_rows, :]] * (n + 1), axis=1)
        block = step_pair(block, all_open, own_speeds)
        tiles = [block[:, t * LANES : (t + 1) * LANES] for t in range(n + 1)]
        for t in range(n):
            sent[t, rows, :] = tiles[t]
            edge = jnp.where(lane < 64, tiles[t + 1], tiles[t - 1])
            if g:
                edge = pltpu.roll(edge, 8 * g, 1)
                mine = (lane >= 8 * g - 4) & (lane < 8 * g + 4)
                edge = jnp.where(mine, edge, sent[t, depth : depth + 8, :])
            sent[t, depth : depth + 8, :] = edge

    def first(dest, source):
        return pltpu.make_async_remote_copy(
            src_ref=sent.at[dest], dst_ref=got.at[source],
            send_sem=send_one.at[dest], recv_sem=recv_one.at[source],
            device_id={"cell": dest}, device_id_type=MESH,
        )

    pl.semaphore_wait(barrier, n - 1)

    def push(k, _):
        first(lax.rem(me + n - k, n), me).start()
        return 0

    lax.fori_loop(1, n, push, 0)

    main_sea = sea[:, pl.ds(pl.multiple_of(me * LANES, LANES), LANES)]
    next_sea = sea[:, pl.ds(pl.multiple_of((me + 1) * LANES, LANES), LANES)]
    last_tile = lax.rem(me + n, n + 1)
    last_sea = sea[:, pl.ds(pl.multiple_of(last_tile * LANES, LANES), LANES)]
    side_sea = jnp.where(lane < 4, next_sea, jnp.where(lane >= LANES - 4, last_sea, 0.0))
    near_sea = jnp.concatenate([main_sea, side_sea], axis=1)
    near_open = (near_sea * pltpu.roll(near_sea, 2 * LANES - 1, 1))[0:1, :]

    def unpack(source, block):
        halo = (lane < 4) | (lane >= LANES - 4)
        edge = block[depth : depth + 8, :]
        for g in range(packs):
            rows = pl.ds(pl.multiple_of(source * depth + g * 8, 8), 8)
            state[rows, 0:LANES] = block[g * 8 : g * 8 + 8, :]
            turned = pltpu.roll(edge, LANES - 8 * g, 1) if g else edge
            state[rows, LANES:] = jnp.where(halo, turned, 0.0)

    unpack(me, sent[me])

    def pull(k, _):
        source = lax.rem(me + k, n)
        first(source, source).wait_recv()
        unpack(source, got[source])
        return 0

    lax.fori_loop(1, n, pull, 0)

    wide = 64

    def narrow(i, _):
        rows = pl.ds(pl.multiple_of(i * wide, wide), wide)
        rounded[rows, :] = state[rows, :].astype(jnp.bfloat16)
        return 0

    lax.fori_loop(0, comps // wide, narrow, 0)

    mode_part, comp_part = modes // 2, comps // 4

    def lifting(width):
        def body(i, _):
            rows = pl.ds(pl.multiple_of(i * mode_part, mode_part), mode_part)
            lifted = jnp.dot(
                lift[rows, :], rounded[:, :width], preferred_element_type=jnp.float32
            )
            squared[rows, :width] = (lifted * lifted).astype(jnp.bfloat16)
            return 0

        lax.fori_loop(0, 2, body, 0)

    load_lift.wait()
    lifting(2 * LANES)
    load_back.wait()

    def source_one(i, _):
        rows = pl.ds(pl.multiple_of(i * comp_part, comp_part), comp_part)
        source = jnp.dot(back[rows, :], squared[...], preferred_element_type=jnp.float32)
        state[rows, :] = state[rows, :] + coupling * source
        return 0

    lax.fori_loop(0, 4, source_one, 0)

    slab, piece = 128, 32
    near_open = jnp.broadcast_to(near_open, (piece, 2 * LANES))

    def propagate(i, _):
        spans = [
            pl.ds(pl.multiple_of(i * slab + j * piece, piece), piece) for j in range(slab // piece)
        ]
        before = [state[rows, :] for rows in spans]
        after = [
            step_pair(block, near_open, jnp.concatenate([speeds[rows, :]] * 2, axis=1))
            for rows, block in zip(spans, before)
        ]
        for rows, block in zip(spans, after):
            state[rows, 0:LANES] = block[:, :LANES]
            rounded[rows, 0:LANES] = block[:, :LANES].astype(jnp.bfloat16)
        return 0

    lax.fori_loop(0, comps // slab, propagate, 0)
    lifting(LANES)

    def place(source):
        return out_ref.at[source]

    def second(dest, source):
        return pltpu.make_async_remote_copy(
            src_ref=result.at[dest], dst_ref=place(source),
            send_sem=send_two.at[dest], recv_sem=recv_two.at[source],
            device_id={"cell": dest}, device_id_type=MESH,
        )

    own = pltpu.make_async_copy(result.at[me], place(me), own_sem)
    part = n // 4

    def source_two(step, _):
        i = lax.rem(me // part + 1 + step, 4)
        rows = pl.ds(pl.multiple_of(i * comp_part, comp_part), comp_part)
        source = jnp.dot(
            back[rows, :], squared[:, :LANES], preferred_element_type=jnp.float32
        )
        total = state[rows, 0:LANES] + coupling * source
        result[pl.ds(i * part, part)] = total.reshape(part, depth, LANES)

        def send(j, _):
            dest = i * part + j

            @pl.when(dest != me)
            def _():
                second(dest, me).start()

            return 0

        lax.fori_loop(0, part, send, 0)
        return 0

    lax.fori_loop(0, 4, source_two, 0)
    own.start()

    def finish(k, _):
        dest = lax.rem(me + k, n)
        source = lax.rem(me + n - k, n)
        first(dest, me).wait_send()
        second(dest, me).wait_send()
        second(source, source).wait_recv()
        return 0

    lax.fori_loop(1, n, finish, 0)
    own.wait()


def shards(wave_energy, courant, sea_mask, lift_weight, back_weight):
    n = lax.axis_size("cell")
    groups, cells = wave_energy.shape
    modes = lift_weight.shape[0]
    depth = -(-groups // 8) * 8
    extra = depth - groups
    if extra:
        wave_energy = jnp.pad(wave_energy, ((0, extra), (0, 0)))
        courant = jnp.pad(courant.reshape(n, groups), ((0, 0), (0, extra))).reshape(-1)
        lift_weight = jnp.pad(
            lift_weight.reshape(modes, n, groups), ((0, 0), (0, 0), (0, extra))
        ).reshape(modes, n * depth)
        back_weight = jnp.pad(
            back_weight.reshape(n, groups, modes), ((0, 0), (0, extra), (0, 0))
        ).reshape(n * depth, modes)
    comps = n * depth
    speed_rows = jnp.pad(courant, (0, -comps % LANES)).reshape(-1, LANES)
    vmem = pl.BlockSpec(memory_space=pltpu.VMEM)
    anywhere = pl.BlockSpec(memory_space=pl.ANY)
    out = pl.pallas_call(
        functools.partial(kernel, n),
        out_shape=jax.ShapeDtypeStruct((n, depth, cells // n), jnp.float32),
        in_specs=[vmem, vmem, vmem, anywhere, anywhere],
        out_specs=anywhere,
        scratch_shapes=[
            pltpu.VMEM((n, depth + 8, LANES), jnp.float32),
            pltpu.VMEM((n, depth + 8, LANES), jnp.float32),
            pltpu.VMEM((comps, 2 * LANES), jnp.float32),
            pltpu.VMEM((comps, 2 * LANES), jnp.bfloat16),
            pltpu.VMEM((modes, 2 * LANES), jnp.bfloat16),
            pltpu.VMEM((n, depth, LANES), jnp.float32),
            pltpu.VMEM((8, cells + LANES), jnp.float32),
            pltpu.VMEM((speed_rows.size, LANES), jnp.float32),
            pltpu.VMEM((modes, comps), jnp.bfloat16),
            pltpu.VMEM((comps, modes), jnp.bfloat16),
            pltpu.SemaphoreType.DMA((2,)),
            pltpu.SemaphoreType.DMA,
            pltpu.SemaphoreType.DMA((n,)),
            pltpu.SemaphoreType.DMA((n,)),
            pltpu.SemaphoreType.DMA((n,)),
            pltpu.SemaphoreType.DMA((n,)),
        ],
        compiler_params=pltpu.CompilerParams(collective_id=0, has_side_effects=True),
    )(wave_energy, speed_rows, sea_mask[None, :], lift_weight, back_weight)
    return out.transpose(1, 0, 2).reshape(depth, cells)[:groups]


def solution(mesh):
    placed = (P(("member", "cell"), None), P(), P(), P(), P())
    return jax.shard_map(
        shards, mesh=mesh, in_specs=placed, out_specs=P(("member", "cell"), None), check_vma=False
    )
```
